32 devices in a mesh: groups: 2 (over x), owner: 16 (over z, y, core).
Axes of the slice: x: 2, y: 2, z: 4, core: 2. Of those that a mesh axis runs over, the one named last changes fastest.
Arguments:
- queries: bfloat16 [512, 8192], P(('groups', 'owner')), parts along dimension 0, may hold values from -12 to 12
- request_prefix: int32 [512, 1], P(('groups', 'owner')), parts along dimension 0, may hold values from 0 to 15; in each aligned block of 16 rows (0 to 15, 16 to 31, ...) at most 2 rows name the same one
- suffix_len: int32 [512], P(('groups', 'owner')), parts along dimension 0, may hold values from 1 to 32, 4096 in all
- block_map: int32 [64], P('groups'), parts along dimension 0, may hold values from 0 to 31, each once
- prefix_keys: bfloat16 [64, 1024, 1024], P(('groups', 'owner')), parts along dimension 0, may hold values from -12 to 12
- prefix_values: bfloat16 [64, 1024, 1024], P(('groups', 'owner')), parts along dimension 0, may hold values from -10 to 10
- suffix_keys: bfloat16 [512, 32, 1024], P(('groups', 'owner')), parts along dimension 0, may hold values from -12 to 12
- suffix_values: bfloat16 [512, 32, 1024], P(('groups', 'owner')), parts along dimension 0, may hold values from -10 to 10
Outputs:
- attended: bfloat16 [512, 8192], P(('groups', 'owner')), parts along dimension 0
The draws below stay inside these ranges and needn't reach their ends.
There are 2 independent parts, one for each index of `groups`. The reference program is written for one: setup_inputs(seed, part) draws one part's arguments, and reference() takes and returns one part's arrays. A program takes and returns all parts, laid end to end along the dimension named above; each array names one. Nothing has to cross between parts.
Inputs may be any that keep to these rules, and one draw needn't show every extreme that they name: `request_prefix`: at most 2 requests of one device continue the same prefix. `block_map`: each slot appears once; slot s lies on owner s // 2.
All inputs are finite; a program needn't handle non-finite values. No bound on the sum of `suffix_len` on one device may be relied on, other than what follows from the above.
Results may differ from the reference program's by a relative error of at most 0.0043.
Values may be sent and summed in bfloat16 or wider, within the bound.
No kernel may reach another device: no remote copies, remote signals or barrier semaphores. Data moves between devices by JAX's collectives and lax.ppermute only.
A program may use at most 128 MiB of HBM per device.

```python
import math
import jax
import jax.numpy as jnp
import numpy as np
from jax import lax

HEADS = 64
KV_HEADS = 8
HEAD_DIM = 128
REQ_DEV = 16
SPAN = 1024
PREFIXES = 16
CAP = 2
SUF = 32
REQUESTS = 256
SLOTS = 32
CPP = 2


def draw_queries(key, part):
    shape = (REQUESTS, HEADS * HEAD_DIM)
    noise = 1.5 * jax.random.normal(jax.random.fold_in(key, 103), shape, jnp.float32)
    return jnp.clip(noise, -12.0, 12.0).astype(jnp.bfloat16)


def draw_prefix_keys(key, part):
    shape = (SLOTS, SPAN, KV_HEADS * HEAD_DIM)
    noise = 1.5 * jax.random.normal(jax.random.fold_in(key, 203), shape, jnp.float32)
    return jnp.clip(noise, -12.0, 12.0).astype(jnp.bfloat16)


def steps_of(own_key, shape, cuts, low, largest):
    loudness, own = 1.0, jax.random.fold_in(own_key, 6)
    for axis_at, shards_of in cuts:
        steps = jnp.exp(jax.random.uniform(jax.random.fold_in(own, axis_at), (shards_of,), jnp.float32, low / len(cuts), largest / len(cuts)))
        loudness = loudness * jnp.repeat(steps, shape[axis_at] // shards_of).reshape([-1 if axis == axis_at else 1 for axis in range(len(shape))])
    return loudness


def length_profile(number_of, total, reach, slope):
    loads = [(1 << 20) // math.isqrt(standing ** slope) + 1 for standing in range(2, number_of + 1)]
    surplus, given = total - reach - (number_of - 1), [1] * (number_of - 1)
    while surplus > 0:
        candidates = [i for i in range(number_of - 1) if given[i] < reach]
        whole, remaining = sum([loads[i] for i in candidates]), surplus
        for i in candidates:
            addition = min(reach - given[i], max(1, remaining * loads[i] // whole), surplus)
            given[i] = given[i] + addition
            surplus = surplus - addition
    return np.array([reach] + given)


def ragged(own_key, amount, total, most, lean):
    if amount == 2:
        one = jax.random.randint(own_key, (), max(1, total - most), min(most, total - 1) + 1)
        return jnp.stack([one, total - one])
    tallies = jnp.asarray(length_profile(amount, total, most, lean), jnp.int32)
    twos = (amount - 1) // 2
    giver, taker = tallies[1:1 + 2 * twos:2], tallies[2:2 + 2 * twos:2]
    room = jnp.minimum(giver - 1, most - taker)
    moved = jax.random.randint(jax.random.fold_in(own_key, 1), (twos,), 0, 1 << 20) % (room + 1)
    tallies = tallies.at[1:1 + 2 * twos:2].set(giver - moved).at[2:2 + 2 * twos:2].set(taker + moved)
    return tallies[jax.random.permutation(jax.random.fold_in(own_key, 2), amount)]


def deal_out(key, own, number, rows, count, top, most, lean):
    ranking = jax.random.permutation(key, count)
    packed, common = portions_of(count, rows * top, most, lean, True), portions_of(count, rows * top, most, lean, False)
    places = jnp.arange(count)

    def named(sizes, rotation):
        used = int((sizes > 0).sum())
        fixed = max(1, used // 4)
        shifted = fixed + (places - fixed + rotation * (used - fixed)) % max(1, count - fixed)
        return jnp.zeros((count,), jnp.int32).at[ranking[jnp.where(places < fixed, places, shifted)]].set(jnp.asarray(sizes, jnp.int32))

    sizes = jnp.where(number % 4 == 0, named(packed, number // 4), named(common, number - number // 4 - 1))
    mixed = jax.random.permutation(jax.random.fold_in(own, 3), count)
    donor, receiver = mixed[0:count // 2 * 2:2], mixed[1:count // 2 * 2:2]
    room = jnp.minimum(sizes[donor] - 1, most - sizes[receiver]) // 2
    room = jnp.where((donor == ranking[0]) | (receiver == ranking[0]) | (sizes[receiver] == 0), 0, jnp.maximum(room, 0))
    shifted = jax.random.randint(jax.random.fold_in(own, 4), (count // 2,), 0, 1 << 20) % (room + 1)
    sizes = sizes.at[donor].add(-shifted).at[receiver].add(shifted)
    labels = jnp.searchsorted(jnp.cumsum(sizes), jnp.arange(rows * top), side="right").astype(jnp.int32)
    grid = labels.reshape(top, rows).T
    grid = grid[jax.random.permutation(jax.random.fold_in(own, 1), rows)]
    rotation = jax.random.randint(jax.random.fold_in(own, 2), (rows, 1), 0, top)
    return jnp.take_along_axis(grid, (jnp.arange(top)[None, :] + rotation) % top, axis=1)


def portions_of(number_of, total, reach, slope, full):
    portions = [(1 << 20) // math.isqrt(grade ** slope) + 1 for grade in range(1, number_of + 1)]
    largest = reach if full else min(reach, max(-(-total // number_of), total * portions[0] // sum(portions)))
    least = 1 if total - largest >= number_of - 1 else 0
    counts, spare = [largest] + [least] * (number_of - 1), total - largest - least * (number_of - 1)
    while spare > 0:
        candidates = [i for i in range(1, number_of) if counts[i] < largest] or [i for i in range(1, number_of) if counts[i] < reach]
        pool, remaining = sum([portions[i] for i in candidates]), spare
        for i in candidates:
            more = min(reach - counts[i], max(1, remaining * portions[i] // pool), spare)
            counts[i] = counts[i] + more
            spare = spare - more
    return np.array(counts)


def normal_values(key, shape, spread, most, pieces=(), held_as=jnp.bfloat16):
    loudness = steps_of(key, shape, pieces, -0.22, 0.18) if pieces else 1.0
    entries = jax.random.normal(key, shape, jnp.float32) * spread * loudness
    return jnp.minimum(jnp.maximum(entries, -most), most).astype(held_as)


def setup_inputs(seed: int = 0, part: int = 0) -> dict:
    arg_keys = jax.random.split(jax.random.key(seed), 9)
    part_keys = jax.random.split(jax.random.fold_in(arg_keys[8], part), 9)
    queries = draw_queries(jax.random.fold_in(jax.random.fold_in(arg_keys[8], part), 71), part)
    request_prefix_keys = jax.random.split(jax.random.fold_in(part_keys[1], 1), REQUESTS // REQ_DEV)
    request_prefix_turns = jax.random.permutation(jax.random.fold_in(part_keys[1], 3), REQUESTS // REQ_DEV)
    request_prefix = jax.vmap(lambda own, number: deal_out(jax.random.fold_in(part_keys[1], 2), own, number, REQ_DEV, PREFIXES, 1, CAP, 2))(request_prefix_keys, request_prefix_turns).reshape((REQUESTS, 1))
    suffix_len = ragged(part_keys[2], REQUESTS, REQUESTS * SUF // 2, SUF, 1).astype(jnp.int32)
    block_map = jax.random.permutation(part_keys[3], SLOTS).astype(jnp.int32)
    prefix_keys = draw_prefix_keys(jax.random.fold_in(jax.random.fold_in(arg_keys[8], part), 71), part)
    prefix_values = normal_values(part_keys[5], (SLOTS, SPAN, KV_HEADS * HEAD_DIM), 2.0, 10.0, ((0, 16),))
    suffix_keys = normal_values(part_keys[6], (REQUESTS, SUF, KV_HEADS * HEAD_DIM), 3.0, 12.0, ((0, 16),))
    suffix_values = normal_values(part_keys[7], (REQUESTS, SUF, KV_HEADS * HEAD_DIM), 2.0, 10.0, ((0, 16),))
    return dict(queries=queries, request_prefix=request_prefix, suffix_len=suffix_len, block_map=block_map, prefix_keys=prefix_keys, prefix_values=prefix_values, suffix_keys=suffix_keys, suffix_values=suffix_values)


NEG_FILL = -1e+30

def prefix_terms(query_row, prefix_id, block_map, prefix_keys, prefix_values):
    per_group = HEADS // KV_HEADS
    span_ids = (prefix_id * CPP + jnp.arange(CPP, dtype=jnp.int32)).astype(jnp.int32)
    slot_ids = jnp.take(block_map, span_ids).astype(jnp.int32)
    key_block = jnp.take(prefix_keys, slot_ids, axis=0).astype(jnp.float32).reshape(CPP, SPAN, KV_HEADS, HEAD_DIM)
    value_block = jnp.take(prefix_values, slot_ids, axis=0).astype(jnp.float32).reshape(CPP, SPAN, KV_HEADS, HEAD_DIM)
    query_heads = query_row.astype(jnp.float32).reshape(KV_HEADS, per_group, HEAD_DIM)
    scores = jnp.einsum('hgd,cthd->chgt', query_heads, key_block) * (1.0 / math.sqrt(HEAD_DIM))
    highest = lax.optimization_barrier(jnp.max(scores, axis=-1, keepdims=True))
    expon = jnp.exp(scores - highest)
    summed = lax.optimization_barrier(jnp.sum(expon, axis=-1))
    weights = lax.optimization_barrier(expon.astype(jnp.bfloat16)).astype(jnp.float32)
    mixed = jnp.einsum('chgt,cthd->chgd', weights, value_block) / summed[..., None]
    span_out = mixed.astype(jnp.bfloat16).reshape(CPP, HEADS, HEAD_DIM)
    span_lse = (highest[..., 0] + jnp.log(summed)).reshape(CPP, HEADS)
    return (span_out, span_lse)

def suffix_terms(queries, suffix_keys, suffix_values, suffix_len):
    row_count = queries.shape[0]
    per_group = HEADS // KV_HEADS
    query_heads = queries.astype(jnp.float32).reshape(row_count, KV_HEADS, per_group, HEAD_DIM)
    key_heads = suffix_keys.astype(jnp.float32).reshape(row_count, SUF, KV_HEADS, HEAD_DIM)
    value_heads = suffix_values.astype(jnp.float32).reshape(row_count, SUF, KV_HEADS, HEAD_DIM)
    scores = jnp.einsum('rhgd,rthd->rhgt', query_heads, key_heads) * (1.0 / math.sqrt(HEAD_DIM))
    visible = (jnp.arange(SUF, dtype=jnp.int32)[None, :] < suffix_len[:, None])[:, None, None, :]
    highest = lax.optimization_barrier(jnp.max(jnp.where(visible, scores, NEG_FILL), axis=-1, keepdims=True))
    expon = jnp.where(visible, jnp.exp(scores - highest), 0.0)
    summed = lax.optimization_barrier(jnp.sum(expon, axis=-1))
    weights = lax.optimization_barrier(expon.astype(jnp.bfloat16)).astype(jnp.float32)
    mixed = jnp.einsum('rhgt,rthd->rhgd', weights, value_heads) / summed[..., None]
    suffix_out = mixed.reshape(row_count, HEADS, HEAD_DIM)
    suffix_lse = (highest[..., 0] + jnp.log(summed)).reshape(row_count, HEADS)
    return (suffix_out, suffix_lse)

def combine_terms(span_out, span_lse, suffix_out, suffix_lse):
    row_count = span_out.shape[0]
    highest = jnp.maximum(lax.optimization_barrier(jnp.max(span_lse, axis=1)), suffix_lse)
    span_scale = jnp.exp(span_lse - highest[:, None, :])
    suffix_scale = jnp.exp(suffix_lse - highest)
    numerator = lax.optimization_barrier(jnp.sum(span_scale[..., None] * span_out.astype(jnp.float32), axis=1)) + suffix_scale[..., None] * suffix_out
    denominator = lax.optimization_barrier(jnp.sum(span_scale, axis=1)) + suffix_scale
    return (numerator / denominator[..., None]).astype(jnp.bfloat16).reshape(row_count, HEADS * HEAD_DIM)

def reference(queries, request_prefix, suffix_len, block_map, prefix_keys, prefix_values, suffix_keys, suffix_values):
    prefix_ids = request_prefix[:, 0].astype(jnp.int32)

    def per_request(pair):
        query_row, prefix_id = pair
        return prefix_terms(query_row, prefix_id, block_map, prefix_keys, prefix_values)
    span_out, span_lse = lax.map(per_request, (queries, prefix_ids))
    suffix_out, suffix_lse = suffix_terms(queries, suffix_keys, suffix_values, suffix_len)
    return combine_terms(span_out, span_lse, suffix_out, suffix_lse)
```

```python
import functools
import math

import jax
import jax.numpy as jnp
from jax import lax
from jax.experimental import pallas as pl
from jax.experimental.pallas import tpu as pltpu
from jax.sharding import PartitionSpec as P

HEADS = 64
KV_HEADS = 8
HEAD_DIM = 128
PREFIXES = 16
CAP = 2

GROUP = HEADS // KV_HEADS
PAIRS = KV_HEADS // 2
FACTOR = 1.0 / math.sqrt(HEAD_DIM)
NEG_FILL = -1e30

BF16 = jnp.bfloat16
F32 = jnp.float32
I32 = jnp.int32

VMEM = pl.BlockSpec(memory_space=pltpu.VMEM)
SMEM = pl.BlockSpec(memory_space=pltpu.SMEM)
ANY = pl.BlockSpec(memory_space=pl.ANY)


def split_pair(tile):
    rows = tile.shape[0]
    wide = tile.astype(F32)
    return [
        wide[:, half * GROUP : (half + 1) * GROUP].reshape(rows * GROUP, HEAD_DIM).astype(BF16)
        for half in range(2)
    ]


def next_cells(prefix_ref, map_ref, count_ref, request, per_prefix, local_slots):
    prefix = prefix_ref[request]
    rank = jnp.minimum(count_ref[prefix], CAP - 1)
    count_ref[prefix] = rank + 1
    cells = []
    for span in range(per_prefix):
        slot = map_ref[prefix * per_prefix + span]
        cells.append((slot // local_slots, (slot % local_slots) * CAP + rank))
    return cells


def clear_counts(count_ref):
    for prefix in range(PREFIXES):
        count_ref[prefix] = 0


def route_kernel(
    per_prefix, local_slots, prefix_ref, map_ref, query_ref, out_ref, rows_ref, stage_ref, count_ref
):
    requests = query_ref.shape[0]
    for head in range(HEADS):
        stage_ref[head * requests : (head + 1) * requests, :] = query_ref[
            :, head * HEAD_DIM : (head + 1) * HEAD_DIM
        ].astype(F32)
    out_ref[...] = jnp.zeros_like(out_ref)
    clear_counts(count_ref)
    for request in range(requests):
        row = stage_ref[pl.ds(request, HEADS, stride=requests), :].astype(BF16)
        rows_ref[request] = row
        for owner, cell in next_cells(
            prefix_ref, map_ref, count_ref, request, per_prefix, local_slots
        ):
            out_ref[owner, cell] = row


def route(queries, prefix, block_map, owners, local_slots):
    requests = queries.shape[0]
    cells = local_slots * CAP
    return pl.pallas_call(
        functools.partial(route_kernel, block_map.shape[0] // PREFIXES, local_slots),
        out_shape=(
            jax.ShapeDtypeStruct((owners, cells, HEADS, HEAD_DIM), BF16),
            jax.ShapeDtypeStruct((requests, HEADS, HEAD_DIM), BF16),
        ),
        in_specs=[SMEM, SMEM, VMEM],
        out_specs=(VMEM, VMEM),
        scratch_shapes=[
            pltpu.VMEM((HEADS * requests, HEAD_DIM), F32),
            pltpu.SMEM((PREFIXES,), I32),
        ],
        name="route",
    )(prefix, block_map, queries)


def span_kernel(rows_ref, key_hbm, value_hbm, out_ref, keys, values, lse_ref, key_sem, value_sem):
    sources, cells = rows_ref.shape[0], rows_ref.shape[1]
    local_slots = key_hbm.shape[0]
    width = 2 * HEAD_DIM
    steps = local_slots * PAIRS

    def fetch(step):
        slot, pair = step // PAIRS, step % PAIRS
        lanes = pl.ds(pair * width, width)
        return (
            pltpu.make_async_copy(key_hbm.at[slot, :, lanes], keys.at[step], key_sem.at[step]),
            pltpu.make_async_copy(value_hbm.at[slot, :, lanes], values.at[step], value_sem.at[step]),
        )

    for step in range(steps):
        for copy in fetch(step):
            copy.start()

    lane = lax.broadcasted_iota(I32, (sources, GROUP, HEAD_DIM), 2)
    room = cells * KV_HEADS
    place = lax.rem(lane, room)
    lse_ref[...] = jnp.zeros_like(lse_ref)

    for step in range(steps):
        slot, pair = step // PAIRS, step % PAIRS
        tile = rows_ref[:, slot * CAP : (slot + 1) * CAP, pair * 2 * GROUP : (pair + 1) * 2 * GROUP, :]
        queries = split_pair(tile.reshape(sources * CAP, 2 * GROUP, HEAD_DIM))
        for copy in fetch(step):
            copy.wait()
        mixed_pair = []
        for half in range(2):
            lanes = slice(half * HEAD_DIM, (half + 1) * HEAD_DIM)
            scores = lax.dot_general(
                queries[half], keys[step, :, lanes], (((1,), (1,)), ((), ())), preferred_element_type=F32
            )
            highest = jnp.max(scores, axis=1, keepdims=True)
            expon = jnp.exp((scores - highest) * FACTOR)
            summed = jnp.sum(expon, axis=1, keepdims=True)
            mixed = jnp.dot(expon.astype(BF16), values[step, :, lanes], preferred_element_type=F32)
            mixed_pair.append((mixed / summed).reshape(sources, CAP, GROUP, HEAD_DIM))
            lse = jnp.broadcast_to(highest * FACTOR + jnp.log(summed), (sources * CAP * GROUP, HEAD_DIM))
            lse = lse.reshape(sources, CAP, GROUP, HEAD_DIM)
            kv_head = pair * 2 + half
            for cap in range(CAP):
                at = (slot * CAP + cap) * KV_HEADS + kv_head
                lse_ref[...] = jnp.where(place == at, lse[:, cap], lse_ref[...])
        both = jnp.concatenate(mixed_pair, axis=2).astype(BF16)
        for cap in range(CAP):
            start = (slot * CAP + cap) * HEADS + pair * 2 * GROUP
            out_ref[:, start : start + 2 * GROUP, :] = both[:, cap]

    lse = lse_ref[...]
    high = lse.astype(BF16).astype(F32)
    middle = (lse - high).astype(BF16).astype(F32)
    low = lse - high - middle
    pieces = jnp.where(lane < room, high, jnp.where(lane < 2 * room, middle, low))
    pieces = jnp.concatenate([pieces, jnp.zeros_like(pieces)], axis=1).astype(BF16)
    out_ref[:, cells * HEADS : cells * HEADS + 2 * GROUP, :] = pieces


def spans(rows, prefix_keys, prefix_values):
    sources, cells = rows.shape[0], rows.shape[1]
    local_slots, tokens = prefix_keys.shape[0], prefix_keys.shape[1]
    steps = local_slots * PAIRS
    area = sources * cells * HEADS * tokens
    return pl.pallas_call(
        span_kernel,
        out_shape=jax.ShapeDtypeStruct((sources, cells * HEADS + 2 * GROUP, HEAD_DIM), BF16),
        in_specs=[VMEM, ANY, ANY],
        out_specs=VMEM,
        scratch_shapes=[
            pltpu.VMEM((steps, tokens, 2 * HEAD_DIM), BF16),
            pltpu.VMEM((steps, tokens, 2 * HEAD_DIM), BF16),
            pltpu.VMEM((sources, GROUP, HEAD_DIM), F32),
            pltpu.SemaphoreType.DMA((steps,)),
            pltpu.SemaphoreType.DMA((steps,)),
        ],
        compiler_params=pltpu.CompilerParams(vmem_limit_bytes=56 << 20),
        cost_estimate=pl.CostEstimate(
            flops=4 * area * HEAD_DIM,
            transcendentals=area,
            bytes_accessed=4 * prefix_keys.size + 4 * rows.size,
        ),
        name="spans",
    )(rows, prefix_keys, prefix_values)


def suffix_kernel(len_ref, query_ref, key_ref, value_ref, out_ref, lse_out_ref, bias_ref):
    requests, room = key_ref.shape[0], key_ref.shape[1]
    column = lax.broadcasted_iota(I32, (GROUP, requests * room), 1)
    for request in range(requests):
        first = request * room
        seen = (column >= first) & (column < first + len_ref[request])
        bias_ref[request * GROUP : (request + 1) * GROUP, :] = jnp.where(seen, 0.0, NEG_FILL)
    lane = lax.broadcasted_iota(I32, (requests, GROUP, HEAD_DIM), 2)
    lse_all = jnp.zeros((requests, GROUP, HEAD_DIM), F32)
    for pair in range(PAIRS):
        queries = split_pair(query_ref[:, pair * 2 * GROUP : (pair + 1) * 2 * GROUP, :])
        for half in range(2):
            kv_head = pair * 2 + half
            lanes = slice(kv_head * HEAD_DIM, (kv_head + 1) * HEAD_DIM)
            key_rows = key_ref[:, :, lanes].reshape(requests * room, HEAD_DIM)
            value_rows = value_ref[:, :, lanes].reshape(requests * room, HEAD_DIM)
            scores = lax.dot_general(
                queries[half], key_rows, (((1,), (1,)), ((), ())), preferred_element_type=F32
            )
            scores = jnp.where(bias_ref[...] < 0.0, NEG_FILL, scores)
            highest = jnp.max(scores, axis=1, keepdims=True)
            expon = jnp.exp((scores - highest) * FACTOR)
            summed = jnp.sum(expon, axis=1, keepdims=True)
            mixed = jnp.dot(expon.astype(BF16), value_rows, preferred_element_type=F32)
            out_ref[:, kv_head * GROUP : (kv_head + 1) * GROUP, :] = (mixed / summed).reshape(
                requests, GROUP, HEAD_DIM
            )
            lse = jnp.broadcast_to(highest * FACTOR + jnp.log(summed), (requests * GROUP, HEAD_DIM))
            lse_all = jnp.where(lane == kv_head, lse.reshape(requests, GROUP, HEAD_DIM), lse_all)
    lse_out_ref[...] = lse_all


def suffixes(rows, suffix_len, suffix_keys, suffix_values):
    requests, room = suffix_keys.shape[0], suffix_keys.shape[1]
    return pl.pallas_call(
        suffix_kernel,
        out_shape=(
            jax.ShapeDtypeStruct((requests, HEADS, HEAD_DIM), F32),
            jax.ShapeDtypeStruct((requests, GROUP, HEAD_DIM), F32),
        ),
        in_specs=[SMEM, VMEM, VMEM, VMEM],
        out_specs=(VMEM, VMEM),
        scratch_shapes=[pltpu.VMEM((requests * GROUP, requests * room), F32)],
        cost_estimate=pl.CostEstimate(
            flops=4 * requests * HEADS * requests * room * HEAD_DIM,
            transcendentals=requests * HEADS * requests * room,
            bytes_accessed=4 * suffix_keys.size + 6 * rows.size,
        ),
        name="suffixes",
    )(suffix_len, rows, suffix_keys, suffix_values)


def combine_kernel(
    per_prefix,
    local_slots,
    prefix_ref,
    map_ref,
    back_ref,
    suffix_ref,
    suffix_lse_ref,
    out_ref,
    stage_ref,
    count_ref,
):
    requests = out_ref.shape[0]
    cells = local_slots * CAP
    room = cells * KV_HEADS
    clear_counts(count_ref)
    for request in range(requests):
        places = next_cells(prefix_ref, map_ref, count_ref, request, per_prefix, local_slots)
        lses = []
        for owner, cell in places:
            pieces = back_ref[owner, cells * HEADS : cells * HEADS + 2 * GROUP, :].astype(F32)[:GROUP]
            pieces = pltpu.roll(pieces, lax.rem(HEAD_DIM - cell * KV_HEADS, HEAD_DIM), 1)
            lses.append(
                pieces
                + pltpu.roll(pieces, HEAD_DIM - room, 1)
                + pltpu.roll(pieces, HEAD_DIM - 2 * room, 1)
            )
        lses.append(suffix_lse_ref[request])
        top = functools.reduce(jnp.maximum, lses)
        scales = [jnp.exp(lse - top) for lse in lses]
        total = functools.reduce(jnp.add, scales)
        weights = [scale / total for scale in scales]
        for pair in range(PAIRS):
            parts = []
            for owner, cell in places:
                start = pl.multiple_of(cell * HEADS + pair * 2 * GROUP, 2 * GROUP)
                parts.append(back_ref[owner, pl.ds(start, 2 * GROUP), :].astype(F32))
            parts.append(suffix_ref[request, pair * 2 * GROUP : (pair + 1) * 2 * GROUP, :])
            for half in range(2):
                kv_head = pair * 2 + half
                mixed = functools.reduce(
                    jnp.add,
                    [
                        weight[:, kv_head : kv_head + 1] * part[half * GROUP : (half + 1) * GROUP]
                        for weight, part in zip(weights, parts)
                    ],
                )
                stage_ref[pl.ds(kv_head * GROUP * requests + request, GROUP, stride=requests), :] = mixed
    for head in range(HEADS):
        out_ref[:, head * HEAD_DIM : (head + 1) * HEAD_DIM] = stage_ref[
            head * requests : (head + 1) * requests, :
        ].astype(BF16)


def combine(back, prefix, block_map, suffix_out, suffix_lse, local_slots):
    requests = suffix_out.shape[0]
    return pl.pallas_call(
        functools.partial(combine_kernel, block_map.shape[0] // PREFIXES, local_slots),
        out_shape=jax.ShapeDtypeStruct((requests, HEADS * HEAD_DIM), BF16),
        in_specs=[SMEM, SMEM, VMEM, VMEM, VMEM],
        out_specs=VMEM,
        scratch_shapes=[
            pltpu.VMEM((HEADS * requests, HEAD_DIM), F32),
            pltpu.SMEM((PREFIXES,), I32),
        ],
        name="combine",
    )(prefix, block_map, back, suffix_out, suffix_lse)


def exchange(blocks):
    return lax.all_to_all(blocks, "owner", split_axis=0, concat_axis=0, tiled=True)


def body(
    queries,
    request_prefix,
    suffix_len,
    block_map,
    prefix_keys,
    prefix_values,
    suffix_keys,
    suffix_values,
):
    owners = lax.axis_size("owner")
    local_slots = prefix_keys.shape[0]
    prefix = request_prefix[:, 0]
    outgoing, rows = route(queries, prefix, block_map, owners, local_slots)
    received = exchange(outgoing)
    suffix_out, suffix_lse = suffixes(rows, suffix_len, suffix_keys, suffix_values)
    back = exchange(spans(received, prefix_keys, prefix_values))
    return combine(back, prefix, block_map, suffix_out, suffix_lse, local_slots)


def solution(mesh):
    placed = (
        P(("groups", "owner"), None),
        P(("groups", "owner"), None),
        P(("groups", "owner")),
        P("groups"),
        P(("groups", "owner"), None, None),
        P(("groups", "owner"), None, None),
        P(("groups", "owner"), None, None),
        P(("groups", "owner"), None, None),
    )
    return jax.shard_map(
        body, mesh=mesh, in_specs=placed, out_specs=P(("groups", "owner"), None), check_vma=False
    )
```
